32 devices in a mesh: groups: 2 (over x), ctx: 16 (over z, y, core).
Axes of the slice: x: 2, y: 2, z: 4, core: 2. Of those that a mesh axis runs over, the one named last changes fastest.
Arguments:
- ssm_input: bfloat16 [8192, 4096], P(('groups', 'ctx')), parts along dimension 0, may hold values from -18 to 18
- gate_input: bfloat16 [8192, 4096], P(('groups', 'ctx')), parts along dimension 0, may hold values from -6 to 6
- bc_input: bfloat16 [8192, 1024], P(('groups', 'ctx')), parts along dimension 0, may hold values from -6 to 6
- dt_raw: float32 [8192, 64], P(('groups', 'ctx')), parts along dimension 0, may hold values from -4 to 16
- offsets: int32 [38], P('groups'), parts along dimension 0, may hold values from 0 to 4096, as said below
- owners: int32 [36], P('groups'), parts along dimension 0, may hold values from 0 to 15, as said below
- conv_weight: float32 [4, 5120], replicated, may hold values from -3 to 3
- convolution_bias: float32 [5120], replicated, may hold values from -3 to 3
- a_log: float32 [64], replicated, may hold values from -3.6 to 2.5
- dt_bias: float32 [64], replicated, may hold values from -6.2 to -5.2
- d_skip: float32 [64], replicated, may hold values from 0.5 to 1.5
- norm_weight: float32 [4096], replicated, may hold values from 0.25 to 1.75
Outputs:
- gated_out: bfloat16 [8192, 4096], P(('groups', 'ctx')), parts along dimension 0
- decode_states: float32 [64, 64, 64, 128], P(('groups', 'ctx')), parts along dimension 0
The draws below stay inside these ranges and needn't reach their ends.
There are 2 independent parts, one for each index of `groups`. The reference program is written for one: setup_inputs(seed, part) draws one part's arguments, and reference() takes and returns one part's arrays. A program takes and returns all parts, laid end to end along the dimension named above; an argument that names none is the same for every part. Nothing has to cross between parts.
Inputs may be any that keep to these rules, and one draw needn't show every extreme that they name: offsets[0] is 0, offsets[18] is 4096 and the offsets rise strictly; every document holds at most 512 tokens and one holds exactly 512; at most 4 documents end on the 256 tokens of one device, and exactly 4 on some device. `owners`: each device owns at most 2 documents, and some device exactly 2.
All inputs are finite; a program needn't handle non-finite values.
Results may differ from the reference program's by a relative error of at most 0.001.
The reference program's roundings to bfloat16 on the way (of `conv_out` and `weights`) count: a program that leaves them out, or rounds other values in their place, can miss the bound.
Values may be sent and summed in bfloat16 or wider, within the bound.
A program may use at most 128 MiB of HBM per device.

```python
import math
import jax
import jax.numpy as jnp
from jax import lax

HEAD_COUNT = 64
HEAD_DIM = 64
STATE_DIM = 128
KERNEL_WIDTH = 4
BLOCK_LEN = 256
END_SLOTS = 4
OWNER_SLOTS = 2
TOK_DEV = 256
GROUP_COUNT = 4
INNER_DIM = 4096
CHANNELS = 5120
GROUP_SEQUENCE = 4096
DOC_COUNT = 18
OWNER_ROWS = 32
N_CTX = 16


def draw_offsets(key, part):
    keys = jax.random.split(key, 4)
    span = N_CTX // 8
    cell_len = TOK_DEV // END_SLOTS
    first_dev = jax.random.randint(keys[0], (), 0, N_CTX - span - 1)
    picked = jax.random.randint(keys[1], (), 0, N_CTX - span - 2)
    dense_dev = jnp.where(picked < first_dev, picked, picked + span + 1)
    last_dev = first_dev + span
    devices = jnp.arange(N_CTX, dtype=jnp.int32)
    cells = jnp.arange(END_SLOTS, dtype=jnp.int32)
    cell_pick = jax.random.randint(keys[2], (N_CTX,), 0, END_SLOTS)
    jitter = jax.random.randint(keys[3], (N_CTX, END_SLOTS), 1, cell_len + 1)
    cell_pick = cell_pick.at[last_dev].set(cell_pick[first_dev])
    jitter = jitter.at[last_dev].set(jitter[first_dev])
    cell_pick = jnp.where(devices == N_CTX - 1, cell_pick % (END_SLOTS - 1), cell_pick)
    inside = (devices > first_dev) & (devices < last_dev)
    single = (cells[None, :] == cell_pick[:, None]) & jnp.logical_not(inside)[:, None]
    flagged = jnp.where((devices == dense_dev)[:, None], True, single)
    places = devices[:, None] * TOK_DEV + cells[None, :] * cell_len + jitter
    flat_flag = flagged.reshape(-1)
    flat_place = places.reshape(-1).astype(jnp.int32)
    order_rank = jnp.cumsum(flat_flag.astype(jnp.int32)) - 1
    target = jnp.where(flat_flag, order_rank, DOC_COUNT - 1)
    inner_cuts = jnp.zeros((DOC_COUNT - 1,), jnp.int32).at[target].set(flat_place, mode='drop')
    return jnp.concatenate([jnp.zeros((1,), jnp.int32), inner_cuts, jnp.full((1,), GROUP_SEQUENCE, jnp.int32)])


def draw_owners(key, part):
    keys = jax.random.split(key, 3)
    shuffled = jax.random.permutation(keys[0], N_CTX).astype(jnp.int32)
    first_pair = jax.random.randint(keys[1], (), 0, DOC_COUNT - 3)
    second_pair = first_pair + 2 + jax.random.randint(keys[2], (), 0, DOC_COUNT - 3 - first_pair)
    doc_ids = jnp.arange(DOC_COUNT, dtype=jnp.int32)
    position = doc_ids - (doc_ids > first_pair).astype(jnp.int32) - (doc_ids > second_pair).astype(jnp.int32)
    return shuffled[position].astype(jnp.int32)


def draw_a_log(key, part):
    keys = jax.random.split(key, 2)
    choose = jax.random.uniform(keys[0], (HEAD_COUNT,))
    level = jax.random.uniform(keys[1], (HEAD_COUNT,))
    share = 0.5
    slow_rate = math.log(0.03) + level * (math.log(0.09) - math.log(0.03))
    fast_rate = math.log(5.0) + level * (math.log(12.0) - math.log(5.0))
    return jnp.where(choose < share, fast_rate, slow_rate).astype(jnp.float32)


def draw_dt_raw(key, part):
    keys = jax.random.split(key, 3)
    block_len = TOK_DEV // 2
    gaussian_perturbation = 0.3 * jax.random.truncated_normal(keys[0], -6.0, 6.0, (GROUP_SEQUENCE, HEAD_COUNT))
    shifts = jax.random.uniform(keys[1], (GROUP_SEQUENCE // block_len,), minval=-0.7, maxval=0.7)
    displaced_lines = jnp.repeat(shifts, block_len)
    sequence_locations = jax.random.randint(keys[2], (max(N_CTX // 8, 1),), 0, GROUP_SEQUENCE)
    sequence_stretch = jnp.any(jnp.arange(GROUP_SEQUENCE)[:, None] == sequence_locations[None, :], 1)
    quantity_elements = gaussian_perturbation + displaced_lines[:, None] + jnp.where(sequence_stretch, 12.5, 0.0)[:, None]
    return quantity_elements.astype(jnp.float32)


def draw_ssm_input(key, part):
    keys = jax.random.split(key, 2)
    columns = jnp.exp(jax.random.uniform(keys[1], (INNER_DIM,), minval=math.log(0.3), maxval=math.log(3.0)))
    quantity_elements = jax.random.truncated_normal(keys[0], -6.0, 6.0, (GROUP_SEQUENCE, INNER_DIM))
    return (quantity_elements * columns[None, :]).astype(jnp.bfloat16)


def levels(own_key, shape, shards, low, top_value):
    loudness = 1.0
    for axis_at, blocks in shards:
        draws = jax.random.uniform(jax.random.fold_in(jax.random.fold_in(own_key, 6), axis_at), (blocks,), jnp.float32, low / len(shards), top_value / len(shards))
        loudness = loudness * jnp.repeat(jnp.exp(draws), shape[axis_at] // blocks).reshape((-1,) + (1,) * (len(shape) - 1 - axis_at))
    return loudness


def noise(own_key, shape, spread, bound, pieces=(), kind=jnp.bfloat16):
    loudness = levels(own_key, shape, pieces, -0.22, 0.18) if pieces else 1.0
    values = jax.random.normal(own_key, shape, jnp.float32) * spread * loudness
    return jnp.minimum(jnp.maximum(values, -bound), bound).astype(kind)


def setup_inputs(seed: int = 0, part: int = 0) -> dict:
    splits = jax.random.split(jax.random.key(seed), 13)
    part_keys = jax.random.split(jax.random.fold_in(splits[12], part), 13)
    return {
        "ssm_input": draw_ssm_input(jax.random.fold_in(jax.random.fold_in(splits[12], part), 71), part),
        "gate_input": noise(part_keys[1], (GROUP_SEQUENCE, INNER_DIM), 1.0, 6.0, ((0, 16),)),
        "bc_input": noise(part_keys[2], (GROUP_SEQUENCE, 2 * GROUP_COUNT * STATE_DIM), 1.0, 6.0, ((0, 16),)),
        "dt_raw": draw_dt_raw(jax.random.fold_in(jax.random.fold_in(splits[12], part), 71), part),
        "offsets": draw_offsets(jax.random.fold_in(jax.random.fold_in(splits[12], part), 71), part),
        "owners": draw_owners(jax.random.fold_in(jax.random.fold_in(splits[12], part), 71), part),
        "conv_weight": noise(splits[6], (KERNEL_WIDTH, CHANNELS), KERNEL_WIDTH ** -0.5, 3.0, (), jnp.float32),
        "convolution_bias": noise(splits[7], (CHANNELS,), 0.5, 3.0, (), jnp.float32),
        "a_log": draw_a_log(jax.random.fold_in(splits[12], 71), part),
        "dt_bias": jnp.clip(jax.random.uniform(splits[9], (HEAD_COUNT,), jnp.float32, -6.2, -5.2), -6.2, -5.2),
        "d_skip": jnp.clip(jax.random.uniform(splits[10], (HEAD_COUNT,), jnp.float32, 0.5, 1.5), 0.5, 1.5),
        "norm_weight": jnp.clip(1.0 + 0.15 * jax.random.normal(splits[11], (INNER_DIM,), jnp.float32), 0.25, 1.75),
    }


def conv_act(conv_in, rim_rows, tok_index, doc_start, conv_weight, convolution_bias):
    length = conv_in.shape[0]
    padded = jnp.concatenate([rim_rows, conv_in], 0)
    total = jnp.zeros(conv_in.shape, jnp.float32) + convolution_bias[None, :]
    for tap_index in range(KERNEL_WIDTH):
        source = tok_index - (KERNEL_WIDTH - 1) + tap_index
        admissible = jnp.where(source >= doc_start, 1.0, 0.0).astype(jnp.float32)
        total = total + admissible[:, None] * conv_weight[tap_index][None, :] * padded[tap_index:tap_index + length].astype(jnp.float32)
    return jax.nn.silu(total).astype(jnp.bfloat16)

def block_terms(ssm_x, b_proj, c_proj, dt_val, log_decay, positions, doc_index, doc_start, slot_end, slot_start, slot_live):
    length, heads, head_dim = ssm_x.shape
    groups = b_proj.shape[1]
    per_group = heads // groups
    slots = slot_end.shape[0]
    cum_decay = jnp.cumsum(log_decay, axis=0)
    scores = jnp.einsum('tgn,sgn->gts', c_proj.astype(jnp.float32), b_proj.astype(jnp.float32), precision=lax.Precision.HIGHEST)
    causal = (positions[None, :] <= positions[:, None]) & (doc_index[None, :] == doc_index[:, None])
    cum_heads = cum_decay.T
    gaps = cum_heads[:, :, None] - cum_heads[:, None, :]
    decay = jnp.exp(jnp.where(causal[None], gaps, -jnp.inf))
    weights = scores[:, None] * decay.reshape(groups, per_group, length, length) * dt_val.T.reshape(groups, per_group, 1, length)
    weights = weights.astype(jnp.bfloat16)
    grouped_x = ssm_x.reshape(length, groups, per_group, head_dim)
    intra = jnp.einsum('gjts,sgjp->tgjp', weights.astype(jnp.float32), grouped_x.astype(jnp.float32), precision=lax.Precision.HIGHEST)
    first_pos = positions[0]
    end_local = jnp.clip(slot_end - first_pos, 0, length - 1)
    cum_end = cum_decay[end_local]
    covered = slot_live[:, None] & (positions[None, :] >= slot_start[:, None]) & (positions[None, :] <= slot_end[:, None])
    slot_decay = jnp.exp(jnp.where(covered[:, :, None], cum_end[:, None, :] - cum_decay[None], -jnp.inf)) * dt_val[None]
    weighted_x = (slot_decay[..., None] * ssm_x[None].astype(jnp.float32)).astype(jnp.bfloat16)
    local = jnp.einsum('iqgjp,qgn->igjpn', weighted_x.reshape(slots, length, groups, per_group, head_dim).astype(jnp.float32), b_proj.astype(jnp.float32), precision=lax.Precision.HIGHEST)
    carried = jnp.where((slot_live & (slot_start < first_pos))[:, None], jnp.exp(cum_end), 0.0).reshape(slots, groups, per_group)
    cont = jnp.where((doc_start < first_pos)[:, None], jnp.exp(cum_decay), 0.0).reshape(length, groups, per_group)
    return (intra, local, carried, cont)

def gate_norm(y_sum, gate_rows, norm_weight):
    length = y_sum.shape[0]
    groups = y_sum.shape[1]
    gated = y_sum.reshape(length, -1) * jax.nn.silu(gate_rows.astype(jnp.float32))
    grouped = gated.reshape(length, groups, -1)
    normed = grouped * lax.rsqrt(lax.optimization_barrier(jnp.mean(grouped * grouped, axis=-1, keepdims=True)) + 1e-05)
    return (normed.reshape(length, -1) * norm_weight[None, :]).astype(jnp.bfloat16)

def reference(ssm_input, gate_input, bc_input, dt_raw, offsets, owners, conv_weight, convolution_bias, a_log, dt_bias, d_skip, norm_weight):
    tok_index = jnp.arange(GROUP_SEQUENCE, dtype=jnp.int32)
    below = offsets[None, :] <= tok_index[:, None]
    doc_index = (lax.optimization_barrier(jnp.sum(below.astype(jnp.int32), 1)) - 1).astype(jnp.int32)
    doc_start = lax.optimization_barrier(jnp.max(jnp.where(below, offsets[None, :], 0), 1)).astype(jnp.int32)
    conv_in = jnp.concatenate([ssm_input, bc_input], 1)
    rim_rows = jnp.zeros((KERNEL_WIDTH - 1, CHANNELS), jnp.bfloat16)
    conv_out = conv_act(conv_in, rim_rows, tok_index, doc_start, conv_weight, convolution_bias)
    group_state = GROUP_COUNT * STATE_DIM
    per_group = HEAD_COUNT // GROUP_COUNT
    ssm_x = conv_out[:, :INNER_DIM].reshape(GROUP_SEQUENCE, HEAD_COUNT, HEAD_DIM)
    b_proj = conv_out[:, INNER_DIM:INNER_DIM + group_state].reshape(GROUP_SEQUENCE, GROUP_COUNT, STATE_DIM)
    c_proj = conv_out[:, INNER_DIM + group_state:].reshape(GROUP_SEQUENCE, GROUP_COUNT, STATE_DIM)
    dt_val = jax.nn.softplus(dt_raw + dt_bias[None, :])
    log_decay = -dt_val * jnp.exp(a_log)[None, :]
    doc_ends = (offsets[1:] - 1).astype(jnp.int32)
    doc_ids = jnp.arange(DOC_COUNT, dtype=jnp.int32)
    earlier = doc_ids[None, :] < doc_ids[:, None]
    owner_rank = lax.optimization_barrier(jnp.sum(((owners[None, :] == owners[:, None]) & earlier).astype(jnp.int32), 1))
    dest_row = (owners * OWNER_SLOTS + owner_rank).astype(jnp.int32)
    slot_ids = jnp.arange(END_SLOTS, dtype=jnp.int32)

    def window_rows(quantity_elements, first):
        return lax.dynamic_slice_in_dim(quantity_elements, first, BLOCK_LEN, 0)

    def run_block(carry, block_index):
        state_in, store = carry
        first = (block_index * BLOCK_LEN).astype(jnp.int32)
        positions = first + jnp.arange(BLOCK_LEN, dtype=jnp.int32)
        in_block = (doc_ends >= first) & (doc_ends < first + BLOCK_LEN)
        order_rank = jnp.cumsum(in_block.astype(jnp.int32)) - 1
        match = (order_rank[None, :] == slot_ids[:, None]) & in_block[None, :]
        slot_live = jnp.any(match, 1)
        slot_doc = lax.optimization_barrier(jnp.sum(match.astype(jnp.int32) * doc_ids[None, :], 1)).astype(jnp.int32)
        slot_end = jnp.where(slot_live, doc_ends[slot_doc], first).astype(jnp.int32)
        slot_start = offsets[slot_doc]
        block_start = window_rows(doc_start, first)
        ext_end = jnp.concatenate([slot_end, jnp.reshape(first + BLOCK_LEN - 1, (1,)).astype(jnp.int32)])
        ext_start = jnp.concatenate([slot_start, block_start[-1:]])
        ext_live = jnp.concatenate([slot_live, jnp.ones((1,), jnp.bool_)])
        x_block = window_rows(ssm_x, first)
        c_block = window_rows(c_proj, first)
        intra, local, carried, cont = block_terms(x_block, window_rows(b_proj, first), c_block, window_rows(dt_val, first), window_rows(log_decay, first), positions, window_rows(doc_index, first), block_start, ext_end, ext_start, ext_live)
        states = local + carried[..., None, None] * state_in[None]
        inter = jnp.einsum('tgn,gjpn->tgjp', c_block.astype(jnp.float32), state_in, precision=lax.Precision.HIGHEST) * cont[..., None]
        skip = d_skip.reshape(GROUP_COUNT, per_group)[None, :, :, None] * x_block.reshape(BLOCK_LEN, GROUP_COUNT, per_group, HEAD_DIM).astype(jnp.float32)
        out_rows = gate_norm(intra + inter + skip, window_rows(gate_input, first), norm_weight)
        for slot_index in range(END_SLOTS):
            target = dest_row[slot_doc[slot_index]]
            current = lax.dynamic_index_in_dim(store, target, 0, keepdims=False)
            update = jnp.where(slot_live[slot_index], states[slot_index].reshape(HEAD_COUNT, HEAD_DIM, STATE_DIM), current)
            store = lax.dynamic_update_index_in_dim(store, update, target, 0)
        return ((states[END_SLOTS], store), out_rows)
    init_state = jnp.zeros((GROUP_COUNT, per_group, HEAD_DIM, STATE_DIM), jnp.float32)
    init_store = jnp.zeros((OWNER_ROWS, HEAD_COUNT, HEAD_DIM, STATE_DIM), jnp.float32)
    carry_out, out_blocks = lax.scan(run_block, (init_state, init_store), jnp.arange(GROUP_SEQUENCE // BLOCK_LEN, dtype=jnp.int32))
    gated_out = out_blocks.reshape(GROUP_SEQUENCE, INNER_DIM)
    return (gated_out, carry_out[1])
```

```python
import functools
import jax
import jax.numpy as jnp
from jax import lax
from jax.experimental import pallas as pl
from jax.experimental.pallas import tpu as pltpu
from jax.sharding import PartitionSpec as P

GROUP_HEADS = 16
KERNEL_WIDTH = 4
OWNER_SLOTS = 2
BLOCK_HEADS = 4
RIM = 8
VMEM_LIMIT = 48 * 1024 * 1024


def shifted(array, axis, by):
    devices = lax.axis_size(axis)
    pairs = [(i, i + by) for i in range(devices) if 0 <= i + by < devices]
    return lax.ppermute(array, axis, pairs)


def conv_silu(x, rim, mask, weight, bias):
    padded = jnp.concatenate([rim, x], 0).astype(jnp.float32)
    total = bias + weight[0:1] * (mask[:, 0:1] * pltpu.roll(padded, 3, 0)[RIM:])
    total = total + weight[1:2] * (mask[:, 1:2] * pltpu.roll(padded, 2, 0)[RIM:])
    total = total + weight[2:3] * (mask[:, 2:3] * pltpu.roll(padded, 1, 0)[RIM:])
    total = total + weight[3:4] * x.astype(jnp.float32)
    return (total / (1.0 + jnp.exp(-total))).astype(jnp.bfloat16)


def conv_kernel(groups, state_dim, x_ref, bc_ref, rim_x_ref, rim_bc_ref, mask_ref, wx_ref, bx_ref, wbc_ref,
                bbc_ref, end_ref, send_ref, c_ref, local_ref, b_scr):
    step = pl.program_id(0)
    width = x_ref.shape[1]
    length = x_ref.shape[0]
    mask = mask_ref[...]

    @pl.when(step == 0)
    def _():
        for part in range(2 * groups):
            cols = slice(part * state_dim, (part + 1) * state_dim)
            value = conv_silu(bc_ref[:, cols], rim_bc_ref[:, cols], mask, wbc_ref[:, cols], bbc_ref[:, cols])
            if part < groups:
                b_scr[part] = value
            else:
                c_ref[:, (part - groups) * state_dim:(part - groups + 1) * state_dim] = value

    xs = conv_silu(x_ref[...], rim_x_ref[...], mask, wx_ref[...], bx_ref[...])
    b_val = b_scr[step * groups // pl.num_programs(0)]
    send_ref[0, :, :width] = xs
    send_ref[0, :, width:] = b_val
    end = end_ref[0]
    heads = end.shape[0]
    x_t = xs.astype(jnp.float32).T.reshape(heads, width // heads, length)
    weighted = (x_t * end[:, None, :]).astype(jnp.bfloat16).reshape(width, length)
    local_ref[0] = jnp.dot(weighted, b_val, preferred_element_type=jnp.float32)


def state_kernel(docs, heads, offsets_ref, dest_ref, recv_ref, cd_ref, out_ref, carry_scr):
    block = pl.program_id(0)
    length = recv_ref.shape[1]
    width = out_ref.shape[1]
    state_dim = out_ref.shape[2]
    head_dim = width // heads

    @pl.when(block == 0)
    def _():
        out_ref[...] = jnp.zeros_like(out_ref)
        carry_scr[...] = jnp.zeros_like(carry_scr)

    first = block * length
    x_t = recv_ref[0, :, :width].astype(jnp.float32).T.reshape(heads, head_dim, length)
    b_val = recv_ref[0, :, width:]
    cum = cd_ref[0, :heads]
    dt = cd_ref[0, heads:]
    lane = lax.broadcasted_iota(jnp.int32, (heads, length), 1)
    incoming = carry_scr[...]

    def state_at(end, start):
        cum_end = jnp.sum(jnp.where(lane == end, cum, 0.0), axis=1, keepdims=True)
        covered = (lane >= start) & (lane <= end)
        weight = jnp.exp(jnp.where(covered, cum_end - cum, -jnp.inf)) * dt
        weighted = (x_t * weight[:, None, :]).astype(jnp.bfloat16).reshape(width, length)
        local = jnp.dot(weighted, b_val, preferred_element_type=jnp.float32)
        factor = jnp.where(start < 0, jnp.exp(cum_end), 0.0)
        return local + (factor[:, :, None] * incoming.reshape(heads, head_dim, state_dim)).reshape(width, state_dim)

    def visit(doc, last_start):
        start = offsets_ref[doc]
        end = offsets_ref[doc + 1] - 1

        @pl.when((end >= first) & (end < first + length))
        def _():
            out_ref[dest_ref[doc]] = state_at(end - first, start - first)

        return jnp.where(start < first + length, start, last_start)

    last_start = lax.fori_loop(0, docs, visit, jnp.int32(0))
    carry_scr[...] = state_at(jnp.int32(length - 1), last_start - first)


def main_kernel(send_ref, c_ref, cum_row_ref, cum_col_ref, cont_ref, dt_row_ref, start_ref, skip_ref, in_ref,
                gate_ref, norm_ref, out_ref, v_scr):
    blocks, length, total = send_ref.shape
    width = skip_ref.shape[1] // blocks
    heads = cum_row_ref.shape[0] // blocks
    head_dim = width // heads
    c_val = c_ref[...]
    contract = (((1,), (1,)), ((), ()))
    scores = lax.dot_general(c_val, send_ref[0, :, width:], contract, preferred_element_type=jnp.float32)
    row = lax.broadcasted_iota(jnp.int32, (length, length), 0)
    col = lax.broadcasted_iota(jnp.int32, (length, length), 1)
    causal = (col <= row) & (col >= start_ref[...])
    part = lax.broadcasted_iota(jnp.int32, (length, width), 1) // head_dim
    square = jnp.zeros((length, 1), jnp.float32)
    for block in range(blocks):
        xs = send_ref[block, :, :width]
        cols = slice(block * width, (block + 1) * width)
        weights, split = [], []
        cont = jnp.zeros((length, width), jnp.float32)
        for head in range(heads):
            at = block * heads + head
            gap = cum_col_ref[0, :, at:at + 1] - cum_row_ref[at:at + 1, :]
            decay = jnp.exp(jnp.where(causal, gap, -jnp.inf))
            weights.append((scores * decay * dt_row_ref[at:at + 1, :]).astype(jnp.bfloat16))
            split.append(jnp.where(part == head, xs, jnp.zeros_like(xs)))
            cont = jnp.where(part == head, cont_ref[0, :, at:at + 1], cont)
        intra = jnp.dot(jnp.concatenate(weights, 1), jnp.concatenate(split, 0), preferred_element_type=jnp.float32)
        state = in_ref[block]
        high = state.astype(jnp.bfloat16)
        low = (state - high.astype(jnp.float32)).astype(jnp.bfloat16)
        inter = lax.dot_general(c_val, high, contract, preferred_element_type=jnp.float32)
        inter = inter + lax.dot_general(c_val, low, contract, preferred_element_type=jnp.float32)
        y_sum = intra + inter * cont + skip_ref[:, cols] * xs.astype(jnp.float32)
        gate = gate_ref[:, cols].astype(jnp.float32)
        value = y_sum * (gate / (1.0 + jnp.exp(-gate)))
        v_scr[:, cols] = value
        square = square + jnp.sum(value * value, axis=1, keepdims=True)
    scale = lax.rsqrt(square / (blocks * width) + 1e-05)
    out_ref[...] = (v_scr[...] * scale * norm_ref[...]).astype(jnp.bfloat16)


def per_device(
    ssm_input,
    gate_input,
    bc_input,
    dt_raw,
    offsets,
    owners,
    conv_weight,
    convolution_bias,
    a_log,
    dt_bias,
    d_skip,
    norm_weight,
):
    length, inner_dim = ssm_input.shape
    heads = a_log.shape[0]
    head_dim = inner_dim // heads
    groups = heads // GROUP_HEADS
    state_dim = bc_input.shape[1] // (2 * groups)
    docs = offsets.shape[0] - 1
    devices = lax.axis_size("ctx")
    blocks = heads // BLOCK_HEADS
    width = BLOCK_HEADS * head_dim
    group_state = groups * state_dim
    channels = inner_dim + 2 * group_state
    base = lax.axis_index("ctx") * length

    tail = jnp.concatenate([ssm_input[length - RIM:], bc_input[length - RIM:]], 1)
    rim = shifted(tail, "ctx", 1)

    local_tok = jnp.arange(length, dtype=jnp.int32)
    tok_index = base + local_tok
    below = offsets[None, :] <= tok_index[:, None]
    doc_start = jnp.max(jnp.where(below, offsets[None, :], 0), 1)
    start_local = doc_start - base
    taps = jnp.arange(KERNEL_WIDTH, dtype=jnp.int32) - (KERNEL_WIDTH - 1)
    mask = jnp.where(local_tok[:, None] + taps[None, :] >= start_local[:, None], 1.0, 0.0).astype(jnp.float32)

    dt = jax.nn.softplus(dt_raw + dt_bias[None, :])
    cum = jnp.cumsum(-dt * jnp.exp(a_log)[None, :], axis=0)
    cum_rows = cum.T
    dt_rows = dt.T
    cum_last = cum_rows[:, length - 1:]
    end_weight = jnp.where(
        (local_tok >= start_local[length - 1])[None, :], jnp.exp(cum_last - cum_rows) * dt_rows, 0.0
    )
    through = jnp.where(start_local[length - 1] < 0, jnp.exp(cum_last), 0.0)
    cont = jnp.where((start_local < 0)[:, None], jnp.exp(cum), 0.0)

    device_heads = heads // devices
    cd_send = jnp.concatenate(
        [cum_rows.reshape(devices, device_heads, length), dt_rows.reshape(devices, device_heads, length)], 1
    )
    cd_recv = lax.all_to_all(cd_send, "ctx", split_axis=0, concat_axis=0, tiled=True)

    full = lambda shape: pl.BlockSpec(shape, lambda j: (0,) * len(shape))
    column = lambda rows: pl.BlockSpec((rows, width), lambda j: (0, j))
    send, c_proj, local_end = pl.pallas_call(
        functools.partial(conv_kernel, groups, state_dim),
        grid=(blocks,),
        in_specs=[
            column(length),
            full((length, 2 * group_state)),
            column(RIM),
            full((RIM, 2 * group_state)),
            full((length, KERNEL_WIDTH)),
            column(KERNEL_WIDTH),
            column(1),
            full((KERNEL_WIDTH, 2 * group_state)),
            full((1, 2 * group_state)),
            pl.BlockSpec((1, BLOCK_HEADS, length), lambda j: (j, 0, 0)),
        ],
        out_specs=[
            pl.BlockSpec((1, length, width + state_dim), lambda j: (j, 0, 0)),
            full((length, group_state)),
            pl.BlockSpec((1, width, state_dim), lambda j: (j, 0, 0)),
        ],
        out_shape=[
            jax.ShapeDtypeStruct((blocks, length, width + state_dim), jnp.bfloat16),
            jax.ShapeDtypeStruct((length, group_state), jnp.bfloat16),
            jax.ShapeDtypeStruct((blocks, width, state_dim), jnp.float32),
        ],
        scratch_shapes=[pltpu.VMEM((groups, length, state_dim), jnp.bfloat16)],
        compiler_params=pltpu.CompilerParams(vmem_limit_bytes=VMEM_LIMIT),
        name="conv",
    )(
        ssm_input,
        bc_input,
        rim[:, :inner_dim],
        rim[:, inner_dim:],
        mask,
        conv_weight[:, :inner_dim],
        convolution_bias[None, :inner_dim],
        conv_weight[:, inner_dim:],
        convolution_bias[None, inner_dim:],
        end_weight.reshape(blocks, BLOCK_HEADS, length),
    )

    device_width = inner_dim // devices
    if devices == blocks:
        outgoing = send
    else:
        share = devices // blocks
        x_part = send[:, :, :width].reshape(blocks, length, share, device_width)
        x_part = x_part.transpose(0, 2, 1, 3).reshape(devices, length, device_width)
        outgoing = jnp.concatenate([x_part, jnp.repeat(send[:, :, width:], share, axis=0)], 2)
    gathered = lax.all_to_all(outgoing, "ctx", split_axis=0, concat_axis=0, tiled=True)

    factor = jnp.repeat(through.reshape(heads), head_dim).reshape(blocks, width, 1)
    incoming = shifted(local_end, "ctx", 1)
    for _ in range(devices // 8 - 1):
        incoming = shifted(factor * incoming + local_end, "ctx", 1)

    doc_ids = jnp.arange(docs, dtype=jnp.int32)
    earlier = doc_ids[None, :] < doc_ids[:, None]
    owner_rank = jnp.sum(((owners[None, :] == owners[:, None]) & earlier).astype(jnp.int32), 1)
    dest_row = owners * OWNER_SLOTS + owner_rank
    rows = devices * OWNER_SLOTS
    states = pl.pallas_call(
        functools.partial(state_kernel, docs, device_heads),
        grid_spec=pltpu.PrefetchScalarGridSpec(
            num_scalar_prefetch=2,
            grid=(devices,),
            in_specs=[
                pl.BlockSpec((1, length, device_width + state_dim), lambda b, *_: (b, 0, 0)),
                pl.BlockSpec((1, 2 * device_heads, length), lambda b, *_: (b, 0, 0)),
            ],
            out_specs=pl.BlockSpec((rows, device_width, state_dim), lambda b, *_: (0, 0, 0)),
            scratch_shapes=[pltpu.VMEM((device_width, state_dim), jnp.float32)],
        ),
        out_shape=jax.ShapeDtypeStruct((rows, device_width, state_dim), jnp.float32),
        compiler_params=pltpu.CompilerParams(vmem_limit_bytes=VMEM_LIMIT),
        name="doc_states",
    )(offsets, dest_row, gathered, cd_recv)
    delivered = lax.all_to_all(
        states.reshape(devices, OWNER_SLOTS * device_width, state_dim), "ctx", split_axis=0, concat_axis=0, tiled=True
    )
    decode_states = (
        delivered.reshape(devices, OWNER_SLOTS, device_heads, head_dim, state_dim)
        .transpose(1, 0, 2, 3, 4)
        .reshape(OWNER_SLOTS, heads, head_dim, state_dim)
    )

    group_blocks = GROUP_HEADS // BLOCK_HEADS
    group_width = group_blocks * width
    per_group = lambda rows: pl.BlockSpec((rows, group_width), lambda g: (0, g))
    by_column = lambda a: a.reshape(length, groups, GROUP_HEADS).transpose(1, 0, 2)
    column_spec = pl.BlockSpec((1, length, GROUP_HEADS), lambda g: (g, 0, 0))
    row_spec = pl.BlockSpec((GROUP_HEADS, length), lambda g: (g, 0))
    gated_out = pl.pallas_call(
        main_kernel,
        grid=(groups,),
        in_specs=[
            pl.BlockSpec((group_blocks, length, width + state_dim), lambda g: (g, 0, 0)),
            pl.BlockSpec((length, state_dim), lambda g: (0, g)),
            row_spec,
            column_spec,
            column_spec,
            row_spec,
            pl.BlockSpec((length, 1), lambda g: (0, 0)),
            per_group(1),
            pl.BlockSpec((group_blocks, width, state_dim), lambda g: (g, 0, 0)),
            per_group(length),
            per_group(1),
        ],
        out_specs=per_group(length),
        out_shape=jax.ShapeDtypeStruct((length, inner_dim), jnp.bfloat16),
        scratch_shapes=[pltpu.VMEM((length, group_width), jnp.float32)],
        compiler_params=pltpu.CompilerParams(vmem_limit_bytes=VMEM_LIMIT),
        cost_estimate=pl.CostEstimate(flops=3_000_000_000, bytes_accessed=12_000_000, transcendentals=6_000_000),
        name="scan_gate_norm",
    )(
        send,
        c_proj,
        cum_rows,
        by_column(cum),
        by_column(cont),
        dt_rows,
        start_local[:, None],
        jnp.repeat(d_skip, head_dim)[None, :],
        incoming,
        gate_input,
        norm_weight[None, :],
    )
    return (gated_out, decode_states)


def solution(mesh):
    in_specs = (
        P(("groups", "ctx"), None),
        P(("groups", "ctx"), None),
        P(("groups", "ctx"), None),
        P(("groups", "ctx"), None),
        P("groups"),
        P("groups"),
        P(),
        P(),
        P(),
        P(),
        P(),
        P(),
    )
    out_specs = (P(("groups", "ctx"), None), P(("groups", "ctx"), None, None, None))
    return jax.shard_map(
        per_device, mesh=mesh, in_specs=in_specs, out_specs=out_specs, check_vma=False
    )
```

```python
import functools
import math
import jax
import jax.numpy as jnp
from jax import lax
from jax.experimental import pallas as pl
from jax.experimental.pallas import tpu as pltpu
from jax.sharding import PartitionSpec as P

GROUP_HEADS = 16
KERNEL_WIDTH = 4
OWNER_SLOTS = 2
BLOCK_HEADS = 4
RIM = 8
SCALE_ROWS = 16
LEVELS = 8.0
CODE_MAX = 32767.0
VMEM_LIMIT = 48 * 1024 * 1024


def shifted(array, axis, by):
    devices = lax.axis_size(axis)
    pairs = [(i, i + by) for i in range(devices) if 0 <= i + by < devices]
    return lax.ppermute(array, axis, pairs)


def encode(value):
    rows, lanes = value.shape
    parts = value.reshape(rows // SCALE_ROWS, SCALE_ROWS, lanes)
    top = jnp.max(jnp.abs(parts), axis=1)
    level = jnp.ceil(jnp.log(jnp.maximum(top, 1e-30)) * (LEVELS / math.log(2.0)))
    unit = jnp.exp2(level * (-1.0 / LEVELS)) * CODE_MAX
    coded = jnp.clip(jnp.round(parts * unit[:, None, :]), -CODE_MAX, CODE_MAX).reshape(rows, lanes)
    if level.shape[0] < SCALE_ROWS:
        level = jnp.concatenate([level, jnp.zeros((SCALE_ROWS - level.shape[0], lanes), jnp.float32)], 0)
    return coded.astype(jnp.int32).astype(jnp.int16), level.astype(jnp.int32).astype(jnp.int16)


def decode(coded, level):
    rows, lanes = coded.shape
    unit = jnp.exp2(level.astype(jnp.int32).astype(jnp.float32) * (1.0 / LEVELS)) * (1.0 / CODE_MAX)
    unit = unit[:rows // SCALE_ROWS]
    parts = coded.astype(jnp.int32).astype(jnp.float32).reshape(rows // SCALE_ROWS, SCALE_ROWS, lanes)
    return (parts * unit[:, None, :]).reshape(rows, lanes)


def conv_silu(x, rim, mask, weight, bias):
    padded = jnp.concatenate([rim, x], 0).astype(jnp.float32)
    total = bias + weight[0:1] * (mask[:, 0:1] * pltpu.roll(padded, 3, 0)[RIM:])
    total = total + weight[1:2] * (mask[:, 1:2] * pltpu.roll(padded, 2, 0)[RIM:])
    total = total + weight[2:3] * (mask[:, 2:3] * pltpu.roll(padded, 1, 0)[RIM:])
    total = total + weight[3:4] * x.astype(jnp.float32)
    return (total / (1.0 + jnp.exp(-total))).astype(jnp.bfloat16)


def conv_kernel(groups, state_dim, x_ref, bc_ref, rim_x_ref, rim_bc_ref, mask_ref, wx_ref, bx_ref, wbc_ref,
                bbc_ref, end_ref, send_ref, c_ref, local_ref, code_ref, b_scr):
    step = pl.program_id(0)
    width = x_ref.shape[1]
    length = x_ref.shape[0]
    mask = mask_ref[...]

    @pl.when(step == 0)
    def _():
        for part in range(2 * groups):
            cols = slice(part * state_dim, (part + 1) * state_dim)
            value = conv_silu(bc_ref[:, cols], rim_bc_ref[:, cols], mask, wbc_ref[:, cols], bbc_ref[:, cols])
            if part < groups:
                b_scr[part] = value
            else:
                c_ref[:, (part - groups) * state_dim:(part - groups + 1) * state_dim] = value

    xs = conv_silu(x_ref[...], rim_x_ref[...], mask, wx_ref[...], bx_ref[...])
    b_val = b_scr[step * groups // pl.num_programs(0)]
    send_ref[0, :, :width] = xs
    send_ref[0, :, width:] = b_val
    end = end_ref[0]
    heads = end.shape[0]
    x_t = xs.astype(jnp.float32).T.reshape(heads, width // heads, length)
    weighted = (x_t * end[:, None, :]).astype(jnp.bfloat16).reshape(width, length)
    local = jnp.dot(weighted, b_val, preferred_element_type=jnp.float32)
    local_ref[0] = local
    code_ref[0, :width], code_ref[0, width:] = encode(local)


def relay_kernel(code_ref, local_ref, factor_ref, out_ref):
    width = local_ref.shape[1]
    value = factor_ref[0] * decode(code_ref[0, :width], code_ref[0, width:]) + local_ref[0]
    out_ref[0, :width], out_ref[0, width:] = encode(value)


def deliver_kernel(code_ref, out_ref):
    slots, heads, head_dim, state_dim = out_ref.shape
    width = heads * head_dim
    for slot in range(slots):
        value = decode(code_ref[0, slot, :width], code_ref[0, slot, width:])
        out_ref[slot] = value.reshape(heads, head_dim, state_dim)


def state_kernel(docs, heads, offsets_ref, dest_ref, recv_ref, cd_ref, mask_ref, weight_ref, bias_ref, out_ref,
                 carry_scr, rim_scr):
    block = pl.program_id(0)
    length = recv_ref.shape[1]
    state_dim = out_ref.shape[2]
    width = out_ref.shape[1] - SCALE_ROWS
    head_dim = width // heads

    @pl.when(block == 0)
    def _():
        out_ref[...] = jnp.zeros_like(out_ref)
        carry_scr[...] = jnp.zeros_like(carry_scr)
        rim_scr[...] = jnp.zeros_like(rim_scr)

    first = block * length
    raw = recv_ref[0]
    conv = conv_silu(raw, rim_scr[...], mask_ref[...], weight_ref[...], bias_ref[...])
    rim_scr[...] = raw[length - RIM:]
    x_t = conv[:, :width].astype(jnp.float32).T.reshape(heads, head_dim, length)
    b_val = conv[:, width:]
    cum = cd_ref[0, :heads]
    dt = cd_ref[0, heads:]
    lane = lax.broadcasted_iota(jnp.int32, (heads, length), 1)

    def state_at(end, start):
        cum_end = jnp.sum(jnp.where(lane == end, cum, 0.0), axis=1, keepdims=True)
        covered = (lane >= start) & (lane <= end)
        weight = jnp.exp(jnp.where(covered, cum_end - cum, -jnp.inf)) * dt
        weighted = (x_t * weight[:, None, :]).astype(jnp.bfloat16).reshape(width, length)
        local = jnp.dot(weighted, b_val, preferred_element_type=jnp.float32)
        factor = jnp.where(start < 0, jnp.exp(cum_end), 0.0)
        carried = factor[:, :, None] * carry_scr[...].reshape(heads, head_dim, state_dim)
        return local + carried.reshape(width, state_dim)

    def visit(doc, last_start):
        start = offsets_ref[doc]
        end = offsets_ref[doc + 1] - 1

        @pl.when((end >= first) & (end < first + length))
        def _():
            row = dest_ref[doc]
            out_ref[row, :width], out_ref[row, width:] = encode(state_at(end - first, start - first))

        return jnp.where(start < first + length, start, last_start)

    last_start = lax.fori_loop(0, docs, visit, jnp.int32(0))
    carry_scr[...] = state_at(jnp.int32(length - 1), last_start - first)


def main_kernel(send_ref, c_ref, cum_row_ref, cum_col_ref, cont_ref, dt_row_ref, start_ref, skip_ref, in_ref,
                gate_ref, norm_ref, out_ref, v_scr):
    blocks, length, total = send_ref.shape
    width = skip_ref.shape[1] // blocks
    heads = cum_row_ref.shape[0] // blocks
    head_dim = width // heads
    c_val = c_ref[...]
    contract = (((1,), (1,)), ((), ()))
    scores = lax.dot_general(c_val, send_ref[0, :, width:], contract, preferred_element_type=jnp.float32)
    row = lax.broadcasted_iota(jnp.int32, (length, length), 0)
    col = lax.broadcasted_iota(jnp.int32, (length, length), 1)
    causal = (col <= row) & (col >= start_ref[...])
    part = lax.broadcasted_iota(jnp.int32, (length, width), 1) // head_dim
    square = jnp.zeros((length, 1), jnp.float32)
    for block in range(blocks):
        xs = send_ref[block, :, :width]
        cols = slice(block * width, (block + 1) * width)
        weights, split = [], []
        cont = jnp.zeros((length, width), jnp.float32)
        for head in range(heads):
            at = block * heads + head
            gap = cum_col_ref[0, :, at:at + 1] - cum_row_ref[at:at + 1, :]
            decay = jnp.exp(jnp.where(causal, gap, -jnp.inf))
            weights.append((scores * decay * dt_row_ref[at:at + 1, :]).astype(jnp.bfloat16))
            split.append(jnp.where(part == head, xs, jnp.zeros_like(xs)))
            cont = jnp.where(part == head, cont_ref[0, :, at:at + 1], cont)
        intra = jnp.dot(jnp.concatenate(weights, 1), jnp.concatenate(split, 0), preferred_element_type=jnp.float32)
        state = decode(in_ref[block, :width], in_ref[block, width:])
        high = state.astype(jnp.bfloat16)
        low = (state - high.astype(jnp.float32)).astype(jnp.bfloat16)
        inter = lax.dot_general(c_val, high, contract, preferred_element_type=jnp.float32)
        inter = inter + lax.dot_general(c_val, low, contract, preferred_element_type=jnp.float32)
        y_sum = intra + inter * cont + skip_ref[:, cols] * xs.astype(jnp.float32)
        gate = gate_ref[:, cols].astype(jnp.float32)
        value = y_sum * (gate / (1.0 + jnp.exp(-gate)))
        v_scr[:, cols] = value
        square = square + jnp.sum(value * value, axis=1, keepdims=True)
    scale = lax.rsqrt(square / (blocks * width) + 1e-05)
    out_ref[...] = (v_scr[...] * scale * norm_ref[...]).astype(jnp.bfloat16)


def per_device(
    ssm_input,
    gate_input,
    bc_input,
    dt_raw,
    offsets,
    owners,
    conv_weight,
    convolution_bias,
    a_log,
    dt_bias,
    d_skip,
    norm_weight,
):
    length, inner_dim = ssm_input.shape
    heads = a_log.shape[0]
    head_dim = inner_dim // heads
    groups = heads // GROUP_HEADS
    state_dim = bc_input.shape[1] // (2 * groups)
    docs = offsets.shape[0] - 1
    devices = lax.axis_size("ctx")
    blocks = heads // BLOCK_HEADS
    width = BLOCK_HEADS * head_dim
    group_state = groups * state_dim
    channels = inner_dim + 2 * group_state
    base = lax.axis_index("ctx") * length

    device_width = inner_dim // devices
    device_heads = heads // devices
    b_raw = bc_input[:, :group_state].reshape(length, groups, state_dim)
    outgoing = jnp.concatenate(
        [ssm_input.reshape(length, devices, device_width), jnp.repeat(b_raw, devices // groups, axis=1)], 2
    ).transpose(1, 0, 2)
    gathered = lax.all_to_all(outgoing, "ctx", split_axis=0, concat_axis=0, tiled=True)

    tail = jnp.concatenate([ssm_input[length - RIM:], bc_input[length - RIM:]], 1)
    rim = shifted(tail, "ctx", 1)

    local_tok = jnp.arange(length, dtype=jnp.int32)
    taps = jnp.arange(KERNEL_WIDTH, dtype=jnp.int32) - (KERNEL_WIDTH - 1)

    def start_of(tokens):
        below = offsets[None, :] <= tokens[:, None]
        return jnp.max(jnp.where(below, offsets[None, :], 0), 1)

    def tap_mask(tokens, starts):
        return jnp.where(tokens[:, None] + taps[None, :] >= starts[:, None], 1.0, 0.0).astype(jnp.float32)

    start_local = start_of(base + local_tok) - base
    mask = tap_mask(local_tok, start_local)
    all_tok = jnp.arange(devices * length, dtype=jnp.int32)
    all_mask = tap_mask(all_tok, start_of(all_tok))

    dt = jax.nn.softplus(dt_raw + dt_bias[None, :])
    cum = jnp.cumsum(-dt * jnp.exp(a_log)[None, :], axis=0)
    cum_rows = cum.T
    dt_rows = dt.T
    cum_last = cum_rows[:, length - 1:]
    end_weight = jnp.where(
        (local_tok >= start_local[length - 1])[None, :], jnp.exp(cum_last - cum_rows) * dt_rows, 0.0
    )
    through = jnp.where(start_local[length - 1] < 0, jnp.exp(cum_last), 0.0)
    cont = jnp.where((start_local < 0)[:, None], jnp.exp(cum), 0.0)

    cd_send = jnp.concatenate(
        [cum_rows.reshape(devices, device_heads, length), dt_rows.reshape(devices, device_heads, length)], 1
    )
    cd_recv = lax.all_to_all(cd_send, "ctx", split_axis=0, concat_axis=0, tiled=True)

    code_spec = pl.BlockSpec((1, width + SCALE_ROWS, state_dim), lambda j: (j, 0, 0))
    code_shape = jax.ShapeDtypeStruct((blocks, width + SCALE_ROWS, state_dim), jnp.int16)
    bias_row = convolution_bias[None, :]
    full = lambda shape: pl.BlockSpec(shape, lambda j: (0,) * len(shape))
    after_x = lambda rows: pl.BlockSpec((rows, 2 * group_state), lambda j: (0, inner_dim // (2 * group_state)))
    column = lambda rows: pl.BlockSpec((rows, width), lambda j: (0, j))
    send, c_proj, local_end, local_code = pl.pallas_call(
        functools.partial(conv_kernel, groups, state_dim),
        grid=(blocks,),
        in_specs=[
            column(length),
            full((length, 2 * group_state)),
            column(RIM),
            after_x(RIM),
            full((length, KERNEL_WIDTH)),
            column(KERNEL_WIDTH),
            column(1),
            after_x(KERNEL_WIDTH),
            after_x(1),
            pl.BlockSpec((1, BLOCK_HEADS, length), lambda j: (j, 0, 0)),
        ],
        out_specs=[
            pl.BlockSpec((1, length, width + state_dim), lambda j: (j, 0, 0)),
            full((length, group_state)),
            pl.BlockSpec((1, width, state_dim), lambda j: (j, 0, 0)),
            code_spec,
        ],
        out_shape=[
            jax.ShapeDtypeStruct((blocks, length, width + state_dim), jnp.bfloat16),
            jax.ShapeDtypeStruct((length, group_state), jnp.bfloat16),
            jax.ShapeDtypeStruct((blocks, width, state_dim), jnp.float32),
            code_shape,
        ],
        scratch_shapes=[pltpu.VMEM((groups, length, state_dim), jnp.bfloat16)],
        compiler_params=pltpu.CompilerParams(vmem_limit_bytes=VMEM_LIMIT),
        name="conv",
    )(
        ssm_input,
        bc_input,
        rim,
        rim,
        mask,
        conv_weight,
        bias_row,
        conv_weight,
        bias_row,
        end_weight.reshape(blocks, BLOCK_HEADS, length),
    )

    factor = jnp.repeat(through.reshape(heads), head_dim).reshape(blocks, width, 1)
    incoming = shifted(local_code, "ctx", 1)
    for _ in range(devices // 8 - 1):
        relayed = pl.pallas_call(
            relay_kernel,
            grid=(blocks,),
            in_specs=[
                code_spec,
                pl.BlockSpec((1, width, state_dim), lambda j: (j, 0, 0)),
                pl.BlockSpec((1, width, 1), lambda j: (j, 0, 0)),
            ],
            out_specs=code_spec,
            out_shape=code_shape,
            name="relay",
        )(incoming, local_end, factor)
        incoming = shifted(relayed, "ctx", 1)
    gathered, incoming = lax.optimization_barrier((gathered, incoming))

    mine = lax.axis_index("ctx")
    b_first = inner_dim + (mine * groups // devices) * state_dim
    taps_and_bias = jnp.concatenate([conv_weight, bias_row], 0)
    own_taps = jnp.concatenate(
        [
            lax.dynamic_slice_in_dim(taps_and_bias, mine * device_width, device_width, 1),
            lax.dynamic_slice_in_dim(taps_and_bias, b_first, state_dim, 1),
        ],
        1,
    )

    doc_ids = jnp.arange(docs, dtype=jnp.int32)
    earlier = doc_ids[None, :] < doc_ids[:, None]
    owner_rank = jnp.sum(((owners[None, :] == owners[:, None]) & earlier).astype(jnp.int32), 1)
    dest_row = owners * OWNER_SLOTS + owner_rank
    rows = devices * OWNER_SLOTS
    code_rows = device_width + SCALE_ROWS
    states = pl.pallas_call(
        functools.partial(state_kernel, docs, device_heads),
        grid_spec=pltpu.PrefetchScalarGridSpec(
            num_scalar_prefetch=2,
            grid=(devices,),
            in_specs=[
                pl.BlockSpec((1, length, device_width + state_dim), lambda b, *_: (b, 0, 0)),
                pl.BlockSpec((1, 2 * device_heads, length), lambda b, *_: (b, 0, 0)),
                pl.BlockSpec((length, KERNEL_WIDTH), lambda b, *_: (b, 0)),
                pl.BlockSpec((KERNEL_WIDTH, device_width + state_dim), lambda b, *_: (0, 0)),
                pl.BlockSpec((1, device_width + state_dim), lambda b, *_: (0, 0)),
            ],
            out_specs=pl.BlockSpec((rows, code_rows, state_dim), lambda b, *_: (0, 0, 0)),
            scratch_shapes=[
                pltpu.VMEM((device_width, state_dim), jnp.float32),
                pltpu.VMEM((RIM, device_width + state_dim), jnp.bfloat16),
            ],
        ),
        out_shape=jax.ShapeDtypeStruct((rows, code_rows, state_dim), jnp.int16),
        compiler_params=pltpu.CompilerParams(vmem_limit_bytes=VMEM_LIMIT),
        name="doc_states",
    )(offsets, dest_row, gathered, cd_recv, all_mask, own_taps[:KERNEL_WIDTH], own_taps[KERNEL_WIDTH:])
    delivered = lax.all_to_all(
        states.reshape(devices, OWNER_SLOTS * code_rows, state_dim), "ctx", split_axis=0, concat_axis=0, tiled=True
    )
    decode_states = pl.pallas_call(
        deliver_kernel,
        grid=(devices,),
        in_specs=[pl.BlockSpec((1, OWNER_SLOTS, code_rows, state_dim), lambda j: (j, 0, 0, 0))],
        out_specs=pl.BlockSpec((OWNER_SLOTS, device_heads, head_dim, state_dim), lambda j: (0, j, 0, 0)),
        out_shape=jax.ShapeDtypeStruct((OWNER_SLOTS, heads, head_dim, state_dim), jnp.float32),
        name="deliver",
    )(delivered.reshape(devices, OWNER_SLOTS, code_rows, state_dim))

    group_blocks = GROUP_HEADS // BLOCK_HEADS
    group_width = group_blocks * width
    per_group = lambda rows: pl.BlockSpec((rows, group_width), lambda g: (0, g))
    by_column = lambda a: a.reshape(length, groups, GROUP_HEADS).transpose(1, 0, 2)
    column_spec = pl.BlockSpec((1, length, GROUP_HEADS), lambda g: (g, 0, 0))
    row_spec = pl.BlockSpec((GROUP_HEADS, length), lambda g: (g, 0))
    gated_out = pl.pallas_call(
        main_kernel,
        grid=(groups,),
        in_specs=[
            pl.BlockSpec((group_blocks, length, width + state_dim), lambda g: (g, 0, 0)),
            pl.BlockSpec((length, state_dim), lambda g: (0, g)),
            row_spec,
            column_spec,
            column_spec,
            row_spec,
            pl.BlockSpec((length, 1), lambda g: (0, 0)),
            per_group(1),
            pl.BlockSpec((group_blocks, width + SCALE_ROWS, state_dim), lambda g: (g, 0, 0)),
            per_group(length),
            per_group(1),
        ],
        out_specs=per_group(length),
        out_shape=jax.ShapeDtypeStruct((length, inner_dim), jnp.bfloat16),
        scratch_shapes=[pltpu.VMEM((length, group_width), jnp.float32)],
        compiler_params=pltpu.CompilerParams(vmem_limit_bytes=VMEM_LIMIT),
        cost_estimate=pl.CostEstimate(flops=3_000_000_000, bytes_accessed=12_000_000, transcendentals=6_000_000),
        name="scan_gate_norm",
    )(
        send,
        c_proj,
        cum_rows,
        by_column(cum),
        by_column(cont),
        dt_rows,
        start_local[:, None],
        jnp.repeat(d_skip, head_dim)[None, :],
        incoming,
        gate_input,
        norm_weight[None, :],
    )
    return (gated_out, decode_states)


def solution(mesh):
    in_specs = (
        P(("groups", "ctx"), None),
        P(("groups", "ctx"), None),
        P(("groups", "ctx"), None),
        P(("groups", "ctx"), None),
        P("groups"),
        P("groups"),
        P(),
        P(),
        P(),
        P(),
        P(),
        P(),
    )
    out_specs = (P(("groups", "ctx"), None), P(("groups", "ctx"), None, None, None))
    return jax.shard_map(
        per_device, mesh=mesh, in_specs=in_specs, out_specs=out_specs, check_vma=False
    )
```
